32 devices in a mesh: lines: 2 (over x), tile: 16 (over z, y, core).
Axes of the slice: x: 2, y: 2, z: 4, core: 2. Of those that a mesh axis runs over, the one named last changes fastest.
Arguments:
- traces: bfloat16 [1024, 512, 512], P(('lines', 'tile')), parts along dimension 0, may hold values from -6 to 6
Outputs:
- multiples: bfloat16 [1024, 512, 512], P(('lines', 'tile')), parts along dimension 0
The draws below stay inside these ranges and needn't reach their ends.
There are 2 independent parts, one for each index of `lines`. The reference program is written for one: setup_inputs(seed, part) draws one part's arguments, and reference() takes and returns one part's arrays. A program takes and returns all parts, laid end to end along the dimension named above; each array names one. Nothing has to cross between parts.
All inputs are finite; a program needn't handle non-finite values.
Results may differ from the reference program's by a relative error of at most 0.011.
Values may be sent and summed in bfloat16 or wider, within the bound.
A program may use at most 128 MiB of HBM per device.

```python
import math
import jax
import jax.numpy as jnp
from jax import lax

S = 512
NT = 512
F = 128


def level_of(rng, dims, shards, smallest, high):
    gain, own = 1.0, jax.random.fold_in(rng, 6)
    for dim, shards_of in shards:
        heights = jnp.exp(jax.random.uniform(jax.random.fold_in(own, dim), (shards_of,), jnp.float32, smallest / len(shards), high / len(shards)))
        gain = gain * jnp.repeat(heights, dims[dim] // shards_of).reshape([-1 if axis == dim else 1 for axis in range(len(dims))])
    return gain


def gaussian(own_key, extent, spread, reach, split=(), kind=jnp.bfloat16):
    entries = jax.random.normal(own_key, extent, jnp.float32) * spread
    if len(split) > 0:
        entries = level_of(own_key, extent, split, -0.22, 0.18) * entries
    return jnp.clip(entries, min=-reach, max=reach).astype(kind)


def setup_inputs(seed: int = 0, part: int = 0) -> dict:
    keys = jax.random.split(jax.random.key(seed), 2)
    part_splits = jax.random.split(jax.random.fold_in(keys[1], part), 2)
    return {
        "traces": gaussian(part_splits[0], (S, S, NT), 1.0, 6.0, ((0, 16),)),
    }


def make_tables():
    times = jnp.arange(NT, dtype=jnp.int32)
    freqs = jnp.arange(F, dtype=jnp.int32)
    phase = times[:, None] * freqs[None, :] % NT
    angle = phase.astype(jnp.float32) * (2.0 * math.pi / NT)
    norm = 1.0 / math.sqrt(NT)
    forward = jnp.stack([jnp.cos(angle), -jnp.sin(angle)], axis=-1).reshape(NT, 2 * F) * norm
    weight = jnp.where(freqs == 0, 1.0, 2.0).astype(jnp.float32)
    inverse = jnp.stack([jnp.cos(angle).T * weight[:, None], -jnp.sin(angle).T * weight[:, None]], axis=1)
    inverse = inverse.reshape(2 * F, NT) * norm
    return (forward.astype(jnp.bfloat16), inverse.astype(jnp.bfloat16))

def per_frequency(item):
    eta = 1.0 / math.sqrt(S)
    full = item.astype(jnp.float32)
    recorded = ((full + jnp.swapaxes(full, 1, 2)) * 0.5).astype(jnp.bfloat16)
    real_part = recorded[0].astype(jnp.float32)
    imag_part = recorded[1].astype(jnp.float32)

    def mult(a, b):
        return jnp.dot(a, b, precision=lax.Precision.HIGHEST)
    square_re = mult(real_part, real_part) - mult(imag_part, imag_part)
    square_im = mult(real_part, imag_part) + mult(imag_part, real_part)
    sum_re = (real_part + eta * square_re).astype(jnp.bfloat16)
    sum_im = (imag_part + eta * square_im).astype(jnp.bfloat16)
    sum_re = lax.optimization_barrier(sum_re).astype(jnp.float32)
    sum_im = lax.optimization_barrier(sum_im).astype(jnp.float32)
    pred_re = eta * (mult(real_part, sum_re) - mult(imag_part, sum_im))
    pred_im = eta * (mult(real_part, sum_im) + mult(imag_part, sum_re))
    return jnp.stack([pred_re, pred_im]).astype(jnp.bfloat16)

def reference(traces):
    forward, inverse = make_tables()
    spectrum = jnp.einsum('srt,tk->ksr', traces.astype(jnp.float32), forward.astype(jnp.float32), precision=lax.Precision.HIGHEST)
    spectrum = spectrum.astype(jnp.bfloat16).reshape(F, 2, S, S)
    predicted = lax.map(per_frequency, spectrum)
    flat = predicted.reshape(2 * F, S, S).astype(jnp.float32)
    multiples = jnp.einsum('ksr,kt->srt', flat, inverse.astype(jnp.float32), precision=lax.Precision.HIGHEST)
    return multiples.astype(jnp.bfloat16)
```

```python
import functools
import math

import jax
import jax.numpy as jnp
from jax import lax
from jax.experimental import pallas as pl
from jax.experimental.pallas import tpu as pltpu
from jax.sharding import PartitionSpec as P

S = 512
NT = 512
F = 128
CHUNKS = 4


def make_tables():
    times = jnp.arange(NT, dtype=jnp.int32)
    freqs = jnp.arange(F, dtype=jnp.int32)
    phase = times[:, None] * freqs[None, :] % NT
    angle = phase.astype(jnp.float32) * (2.0 * math.pi / NT)
    norm = 1.0 / math.sqrt(NT)
    forward = jnp.stack([jnp.cos(angle), -jnp.sin(angle)], axis=-1).reshape(NT, 2 * F) * norm
    weight = jnp.where(freqs == 0, 1.0, 2.0).astype(jnp.float32)
    inverse = jnp.stack(
        [jnp.cos(angle).T * weight[:, None], -jnp.sin(angle).T * weight[:, None]], axis=1
    )
    inverse = inverse.reshape(2 * F, NT) * norm
    return (forward.astype(jnp.bfloat16), inverse.astype(jnp.bfloat16))


def dot(left, right):
    return jnp.dot(left, right, preferred_element_type=jnp.float32)


def predict_kernel(spec_ref, out_ref):
    count, _, _, rows, _ = spec_ref.shape
    eta = 1.0 / math.sqrt(S)

    def recorded(part):
        full = spec_ref[:, 0, part].astype(jnp.float32).reshape(count * rows, S)
        return ((full + full.T) * 0.5).astype(jnp.bfloat16)

    def put(part, value):
        out_ref[:, 0, part] = value.reshape(count, rows, S).astype(jnp.bfloat16)

    real_part = recorded(0)
    imag_part = recorded(1)
    square_re = dot(real_part, real_part) - dot(imag_part, imag_part)
    sum_re = (real_part.astype(jnp.float32) + eta * square_re).astype(jnp.bfloat16)
    square_im = dot(real_part, imag_part) + dot(imag_part, real_part)
    sum_im = (imag_part.astype(jnp.float32) + eta * square_im).astype(jnp.bfloat16)
    put(0, eta * (dot(real_part, sum_re) - dot(imag_part, sum_im)))
    put(1, eta * (dot(real_part, sum_im) + dot(imag_part, sum_re)))


def predict(grouped):
    count, width, _, rows, _ = grouped.shape
    block = pl.BlockSpec((count, 1, 2, rows, S), lambda k: (0, k, 0, 0, 0))
    return pl.pallas_call(
        predict_kernel,
        grid=(width,),
        in_specs=[block],
        out_specs=block,
        out_shape=jax.ShapeDtypeStruct(grouped.shape, jnp.bfloat16),
        compiler_params=pltpu.CompilerParams(vmem_limit_bytes=40 * 2**20),
        cost_estimate=pl.CostEstimate(
            flops=width * 16 * S**3, bytes_accessed=width * 8 * S * S, transcendentals=0
        ),
        name="predict",
    )(grouped)


def local(traces):
    count = lax.axis_size("tile")
    rows = traces.shape[0]
    chunks = math.gcd(CHUNKS, F // count)
    band = F // chunks
    width = band // count
    forward, inverse = make_tables()
    sent = []
    for c in range(chunks):
        table = lax.slice_in_dim(forward, c * 2 * band, (c + 1) * 2 * band, axis=1)
        part = jnp.einsum("srt,tk->ksr", traces, table, preferred_element_type=jnp.float32)
        part = part.astype(jnp.bfloat16).reshape(count, width, 2, rows, S)
        sent.append(lax.all_to_all(part, "tile", split_axis=0, concat_axis=0, tiled=True))
    back = []
    for c in range(chunks):
        predicted = predict(sent[c])
        back.append(lax.all_to_all(predicted, "tile", split_axis=0, concat_axis=0, tiled=True))
    result = jnp.concatenate([b.reshape(2 * band, rows, S) for b in back], axis=0)
    multiples = jnp.einsum("kab,kt->abt", result, inverse, preferred_element_type=jnp.float32)
    return multiples.astype(jnp.bfloat16)


def solution(mesh):
    return jax.shard_map(
        local,
        mesh=mesh,
        in_specs=(P(("lines", "tile"), None, None),),
        out_specs=P(("lines", "tile"), None, None),
        check_vma=False,
    )
```

```python
import functools
import math

import jax
import jax.numpy as jnp
from jax import lax
from jax.experimental import pallas as pl
from jax.experimental.pallas import tpu as pltpu
from jax.sharding import PartitionSpec as P

S = 512
NT = 512
F = 128


def make_tables():
    times = jnp.arange(NT, dtype=jnp.int32)
    freqs = jnp.arange(F, dtype=jnp.int32)
    phase = times[:, None] * freqs[None, :] % NT
    angle = phase.astype(jnp.float32) * (2.0 * math.pi / NT)
    norm = 1.0 / math.sqrt(NT)
    forward = jnp.stack([jnp.cos(angle), -jnp.sin(angle)], axis=-1).reshape(NT, 2 * F) * norm
    weight = jnp.where(freqs == 0, 1.0, 2.0).astype(jnp.float32)
    inverse = jnp.stack(
        [jnp.cos(angle).T * weight[:, None], -jnp.sin(angle).T * weight[:, None]], axis=1
    )
    inverse = inverse.reshape(2 * F, NT) * norm
    return (forward.astype(jnp.bfloat16), inverse.astype(jnp.bfloat16))


def dot(left, right):
    return jnp.dot(left, right, preferred_element_type=jnp.float32)


def predict_one(spec_ref, out_ref, f):
    count, _, _, rows, _ = spec_ref.shape
    eta = 1.0 / math.sqrt(S)

    def recorded(part):
        full = spec_ref[:, f, part].astype(jnp.float32).reshape(count * rows, S)
        return ((full + full.T) * 0.5).astype(jnp.bfloat16)

    def put(part, value):
        out_ref[:, f, part] = value.reshape(count, rows, S).astype(jnp.bfloat16)

    real_part = recorded(0)
    imag_part = recorded(1)
    square_re = dot(real_part, real_part) - dot(imag_part, imag_part)
    sum_re = (real_part.astype(jnp.float32) + eta * square_re).astype(jnp.bfloat16)
    square_im = dot(real_part, imag_part) + dot(imag_part, real_part)
    sum_im = (imag_part.astype(jnp.float32) + eta * square_im).astype(jnp.bfloat16)
    put(0, eta * (dot(real_part, sum_re) - dot(imag_part, sum_im)))
    put(1, eta * (dot(real_part, sum_im) + dot(imag_part, sum_re)))


def exchange_kernel(
    count, x_ref, out_ref, held, pred, go_send, go_recv, go_own, back_send, back_recv, back_own
):
    width = x_ref.shape[1]
    me = lax.axis_index("tile")

    def partner(i):
        return lax.rem(me + lax.rem(i * 5, count), count)

    barrier = pltpu.get_barrier_semaphore()

    @pl.loop(1, count)
    def _(i):
        pl.semaphore_signal(
            barrier, inc=1, device_id={"tile": partner(i)}, device_id_type=pl.DeviceIdType.MESH
        )

    pl.semaphore_wait(barrier, count - 1)

    def send(source, target, f, send_sem, recv_sem):
        @pl.loop(1, count)
        def _(i):
            peer = partner(i)
            pltpu.make_async_remote_copy(
                src_ref=source.at[peer, f],
                dst_ref=target.at[me, f],
                send_sem=send_sem.at[f],
                recv_sem=recv_sem.at[f],
                device_id={"tile": peer},
                device_id_type=pl.DeviceIdType.MESH,
            ).start()

    def own(source, target, f, sem):
        return pltpu.make_async_copy(source.at[me, f], target.at[me, f], sem.at[f])

    def wait_all(ref, f, sem):
        view = ref.at[pl.ds(0, count - 1), f]
        pltpu.make_async_copy(view, view, sem.at[f]).wait()

    @pl.loop(0, width)
    def _(f):
        own(x_ref, held, f, go_own).start()
        send(x_ref, held, f, go_send, go_recv)

    @pl.loop(0, width)
    def _(f):
        own(x_ref, held, f, go_own).wait()
        wait_all(held, f, go_recv)
        predict_one(held, pred, f)
        keep = own(pred, out_ref, f, back_own)
        keep.start()
        keep.wait()
        send(pred, out_ref, f, back_send, back_recv)

    @pl.loop(0, width)
    def _(f):
        wait_all(x_ref, f, go_send)
        wait_all(pred, f, back_send)
        wait_all(out_ref, f, back_recv)


def exchange_and_predict(grouped, count):
    _, width, _, rows, _ = grouped.shape
    sems = pltpu.SemaphoreType.DMA((width,))
    return pl.pallas_call(
        functools.partial(exchange_kernel, count),
        in_specs=[pl.BlockSpec(memory_space=pl.ANY)],
        out_specs=pl.BlockSpec(memory_space=pl.ANY),
        out_shape=jax.ShapeDtypeStruct(grouped.shape, jnp.bfloat16),
        scratch_shapes=[
            pltpu.VMEM(grouped.shape, jnp.bfloat16),
            pltpu.VMEM(grouped.shape, jnp.bfloat16),
            sems, sems, sems, sems, sems, sems,
        ],
        compiler_params=pltpu.CompilerParams(
            collective_id=0, has_side_effects=True, vmem_limit_bytes=56 * 2**20
        ),
        cost_estimate=pl.CostEstimate(
            flops=width * 16 * S**3, bytes_accessed=width * 8 * S * S, transcendentals=0
        ),
        name="exchange_and_predict",
    )(grouped)


def local(traces):
    count = lax.axis_size("tile")
    rows = traces.shape[0]
    forward, inverse = make_tables()
    spectrum = jnp.einsum("srt,tk->ksr", traces, forward, preferred_element_type=jnp.float32)
    grouped = spectrum.astype(jnp.bfloat16).reshape(count, F // count, 2, rows, S)
    result = exchange_and_predict(grouped, count).reshape(2 * F, rows, S)
    multiples = jnp.einsum("kab,kt->abt", result, inverse, preferred_element_type=jnp.float32)
    return multiples.astype(jnp.bfloat16)


def solution(mesh):
    return jax.shard_map(
        local,
        mesh=mesh,
        in_specs=(P(("lines", "tile"), None, None),),
        out_specs=P(("lines", "tile"), None, None),
        check_vma=False,
    )
```
